32 devices in a mesh: dp: 4 (over y, x), space: 8 (over z, core).
Axes of the slice: x: 2, y: 2, z: 4, core: 2. Of those that a mesh axis runs over, the one named last changes fastest.
Arguments:
- features: bfloat16 [4, 2048, 256], P('dp', 'space'), may hold values from -6 to 6
- neighbours: int32 [4, 27, 2048], P('dp', None, 'space'), may hold values from -1 to 2047, as said below
- parents: int32 [4, 2048], P('dp', 'space'), may hold values from 0 to 511, as said below
- conv_first: bfloat16 [27, 256, 256], replicated, may hold values from -0.078125 to 0.078125
- conv_second: bfloat16 [27, 256, 256], replicated, may hold values from -0.078125 to 0.078125
- gain_first: float32 [256], replicated, may hold values from 0.1 to 1.9
- gain_second: float32 [256], replicated, may hold values from 0.1 to 1.9
- down_weight: bfloat16 [256, 512], replicated, may hold values from -0.375 to 0.375
- cotangent: bfloat16 [4, 512, 512], P('dp', 'space'), may hold values from -6 to 6
Outputs:
- fine_out: bfloat16 [4, 2048, 256], P('dp', 'space')
- coarse: bfloat16 [4, 512, 512], P('dp', 'space')
- down_grad: float32 [256, 512], replicated
The draws below stay inside these ranges and needn't reach their ends.
Inputs may be any that keep to these rules, and one draw needn't show every extreme that they name: `neighbours`: for a site s of the block [d * 256, (d + 1) * 256), every entry is -1 or lies in [(d - 1) * 256, (d + 2) * 256); entry 13 is s itself. The parents of the sites of the block [d * 256, (d + 1) * 256) never decrease along the block and lie in [d * 64, (d + 2) * 64).
All inputs are finite; a program needn't handle non-finite values.
Results may differ from the reference program's by a relative error of at most 0.0057.
Values may be sent and summed in bfloat16 or wider, within the bound.
A program may use at most 64 MiB of HBM per device.

```python
import math
import jax
import jax.numpy as jnp
from jax import lax

CH = 256
CH_OUT = 512
TAPS = 27
SITE_DEV = 256
PAR_DEV = 64
SITES = 2048
PARENTS = 512
WORLDS = 4
N_SPACE = 8


def draw_neighbours(key, part):
    first_key, second_key = jax.random.split(jax.random.fold_in(key, 11))
    site_ids = jnp.arange(SITES, dtype=jnp.int32)
    lowest = (site_ids // SITE_DEV - 1) * SITE_DEV
    offsets = jax.random.randint(first_key, (WORLDS, TAPS, SITES), 0, 3 * SITE_DEV)
    global_ids = lowest[None, None, :] + offsets
    alive = jax.random.randint(second_key, (WORLDS, TAPS, SITES), 0, 10) >= 3
    inside = (global_ids >= 0) & (global_ids < SITES)
    global_ids = jnp.where(alive & inside, global_ids, -1)
    centre = (jnp.arange(TAPS) == 13)[None, :, None]
    return jnp.where(centre, site_ids[None, None, :], global_ids).astype(jnp.int32)


def draw_parents(key, part):
    first_key, second_key = jax.random.split(jax.random.fold_in(key, 23))
    extent = jax.random.randint(first_key, (WORLDS, N_SPACE), PAR_DEV // 2, 2 * PAR_DEV + 1)
    extent = extent.at[:, 0].set(2 * PAR_DEV)
    final = (jnp.arange(N_SPACE) == N_SPACE - 1)[None, :]
    extent = jnp.where(final, jnp.minimum(extent, PAR_DEV), extent)
    draws_raw = jax.random.randint(second_key, (WORLDS, N_SPACE, SITE_DEV), 0, 2 * PAR_DEV)
    offsets = jnp.sort(draws_raw % extent[:, :, None], axis=-1)
    offsets = offsets.at[:, :, -1].set(extent - 1)
    anchor = (jnp.arange(N_SPACE, dtype=jnp.int32) * PAR_DEV)[None, :, None]
    return (anchor + offsets).reshape(WORLDS, SITES).astype(jnp.int32)


def steps_of(stream_key, shape, shards, least, top_value):
    def one(dim, shards_of):
        steps = jax.random.uniform(jax.random.fold_in(jax.random.fold_in(stream_key, 6), dim), (shards_of,), jnp.float32, least / len(shards), top_value / len(shards))
        return jnp.repeat(jnp.exp(steps), shape[dim] // shards_of).reshape((-1,) + (1,) * (len(shape) - dim - 1))

    level = one(*shards[0])
    for cut in shards[1:]:
        level = level * one(*cut)
    return level


def scatter_about(key, dims, deviation, limit, cuts=(), kind=jnp.bfloat16):
    result = jax.random.normal(key, dims, jnp.float32) * deviation
    if len(cuts) > 0:
        result = steps_of(key, dims, cuts, -0.22, 0.18) * result
    return jnp.clip(result, min=-limit, max=limit).astype(kind)


def setup_inputs(seed: int = 0) -> dict:
    keys = jax.random.split(jax.random.key(seed), 10)
    return {
        "features": scatter_about(keys[0], (WORLDS, SITES, CH), 1.0, 6.0, ((0, 4), (1, 8))),
        "neighbours": draw_neighbours(jax.random.fold_in(keys[9], 71), 0),
        "parents": draw_parents(jax.random.fold_in(keys[9], 71), 0),
        "conv_first": scatter_about(keys[3], (TAPS, CH, CH), (TAPS * CH) ** -0.5, 0.078125),
        "conv_second": scatter_about(keys[4], (TAPS, CH, CH), (TAPS * CH) ** -0.5, 0.078125),
        "gain_first": jnp.clip(1.0 + 0.18 * jax.random.normal(keys[5], (CH,), jnp.float32), 0.1, 1.9),
        "gain_second": jnp.clip(1.0 + 0.18 * jax.random.normal(keys[6], (CH,), jnp.float32), 0.1, 1.9),
        "down_weight": scatter_about(keys[7], (CH, CH_OUT), CH ** -0.5, 0.375),
        "cotangent": scatter_about(keys[8], (WORLDS, PARENTS, CH_OUT), 1.0, 6.0, ((0, 4), (1, 8))),
    }


def convolve(field, tap_lists, weights):
    site_rows = field.shape[0]
    padded = jnp.concatenate([field, jnp.zeros((1, field.shape[1]), field.dtype)], axis=0)
    lookup = jnp.where(tap_lists < 0, site_rows, tap_lists).astype(jnp.int32)

    def one_tap(running, inputs):
        rows_now, weight = inputs
        return (running + jnp.dot(padded[rows_now], weight, preferred_element_type=jnp.float32), None)
    start = jnp.zeros((site_rows, weights.shape[2]), jnp.float32)
    running, _ = lax.scan(one_tap, start, (lookup, weights))
    return running

def settle(running, gain):
    inverse = lax.rsqrt(lax.optimization_barrier(jnp.mean(running * running, axis=-1, keepdims=True)) + 1e-05)
    return jax.nn.silu(running * inverse * gain)

def reference(features, neighbours, parents, conv_first, conv_second, gain_first, gain_second, down_weight, cotangent):

    def one_world(inputs):
        field, tap_lists, parent_ids, grad_in = inputs
        middle = settle(convolve(field, tap_lists, conv_first), gain_first).astype(jnp.bfloat16)
        fine_out = (field.astype(jnp.float32) + settle(convolve(middle, tap_lists, conv_second), gain_second)).astype(jnp.bfloat16)
        parent_sums = jax.ops.segment_sum(fine_out.astype(jnp.float32), parent_ids, num_segments=PARENTS)
        counts = jax.ops.segment_sum(jnp.ones(parent_ids.shape, jnp.float32), parent_ids, num_segments=PARENTS)
        pooled = (parent_sums / jnp.maximum(counts, 1.0)[:, None]).astype(jnp.bfloat16)
        coarse = jnp.dot(pooled, down_weight, preferred_element_type=jnp.float32).astype(jnp.bfloat16)
        local_grad = jnp.dot(pooled.T, grad_in, preferred_element_type=jnp.float32)
        return (fine_out, coarse, local_grad)
    fine_out, coarse, grads = lax.map(one_world, (features, neighbours, parents, cotangent))
    down_grad = lax.optimization_barrier(jnp.sum(grads, axis=0)) * (1.0 / math.sqrt(WORLDS * PARENTS))
    return (fine_out, coarse, down_grad)
```

```python
import functools
import math

import jax
import jax.numpy as jnp
from jax import lax
from jax.experimental import pallas as pl
from jax.experimental.pallas import tpu as pltpu
from jax.sharding import PartitionSpec as P

F32 = jnp.float32
BF16 = jnp.bfloat16
MESH = pl.DeviceIdType.MESH


def settle(total, gain):
    inverse = lax.rsqrt(jnp.mean(total * total, axis=-1, keepdims=True) + 1e-05)
    u = total * inverse * gain
    return u / (1.0 + jnp.exp(-u))


def kernel(
    shape,
    features,
    neighbours,
    parents,
    gain_first,
    gain_second,
    first_hbm,
    second_hbm,
    down_hbm,
    cot_hbm,
    fine_out,
    coarse,
    grad,
    window,
    middle,
    select,
    picked,
    first,
    second,
    down,
    cot,
    total,
    sums_out,
    sums_in,
    tally_out,
    tally_in,
    parts,
    landed,
    gathered,
    weight_sem,
    small_sem,
    halo_send,
    halo_recv,
    sum_send,
    sum_recv,
    part_send,
    part_recv,
    all_send,
    all_recv,
):
    n_dp, n_space, taps, group, chunks, stride, scale = shape
    n = n_dp * n_space
    rows = features.shape[0]
    par = cot.shape[0]
    chunk_rows, chunk_cols = parts.shape[1:]
    across = grad.shape[1] // chunk_cols
    me_dp, me = lax.axis_index("dp"), lax.axis_index("space")
    flat = me_dp * n_space + me

    def place(device):
        return (device // n_space, device % n_space)

    barrier = pltpu.get_barrier_semaphore()

    def greet(i, carry):
        pl.semaphore_signal(barrier, inc=1, device_id=place((flat + i) % n), device_id_type=MESH)
        return carry

    lax.fori_loop(1, n, greet, 0)

    span = group * first.shape[1]
    steps = taps // group

    def weight_copy(which, g):
        source, target = ((first_hbm, first), (second_hbm, second))[which]
        cut = pl.ds(g * span, span)
        return pltpu.make_async_copy(source.at[cut], target.at[cut], weight_sem.at[which, g])

    small = [
        pltpu.make_async_copy(down_hbm, down, small_sem.at[0]),
        pltpu.make_async_copy(cot_hbm, cot, small_sem.at[1]),
    ]
    for which in range(2):
        for g in range(steps):
            weight_copy(which, g).start()
    for copy in small:
        copy.start()

    ids = neighbours[...]
    lookup = jnp.where(ids < 0, -1, ids - (me - 1) * rows).astype(F32)
    columns = jnp.transpose(lookup)
    places = lax.broadcasted_iota(jnp.int32, (rows, 3 * rows), 1).astype(F32)
    for t in range(taps):
        hit = columns[:, t : t + 1] == places
        select[t] = jnp.where(hit, 1.0, 0.0).astype(BF16)

    parent_ids = me * par + lax.broadcasted_iota(jnp.int32, (2 * par, rows), 0)
    member = jnp.where(parents[...] == parent_ids, 1.0, 0.0)
    tallies = jnp.sum(member, axis=1, keepdims=True)
    tally_out[...] = jnp.broadcast_to(tallies[par:], tally_out.shape)
    member = member.astype(BF16)

    pl.semaphore_wait(barrier, n - 1)

    has_left, has_right = me > 0, me < n_space - 1

    def halo(buffer, phase, side):
        source = features if buffer is window else buffer.at[pl.ds(rows, rows)]
        return pltpu.make_async_remote_copy(
            src_ref=source,
            dst_ref=buffer.at[pl.ds(2 * rows * (1 - side), rows)],
            send_sem=halo_send.at[phase, side],
            recv_sem=halo_recv.at[phase, side],
            device_id=(me_dp, me + (2 * side - 1)),
            device_id_type=MESH,
        )

    def tally_copy():
        return pltpu.make_async_remote_copy(
            src_ref=tally_out,
            dst_ref=tally_in,
            send_sem=sum_send.at[1],
            recv_sem=sum_recv.at[1],
            device_id=(me_dp, me + 1),
            device_id_type=MESH,
        )

    def sums_copy():
        return pltpu.make_async_remote_copy(
            src_ref=sums_out,
            dst_ref=sums_in,
            send_sem=sum_send.at[0],
            recv_sem=sum_recv.at[0],
            device_id=(me_dp, me + 1),
            device_id_type=MESH,
        )

    def exchange_start(buffer, phase):
        @pl.when(has_left)
        def _():
            halo(buffer, phase, 0).start()

        @pl.when(has_right)
        def _():
            halo(buffer, phase, 1).start()

        @pl.when(jnp.logical_not(has_left))
        def _():
            buffer[:rows] = jnp.zeros((rows, buffer.shape[1]), BF16)

        @pl.when(jnp.logical_not(has_right))
        def _():
            buffer[2 * rows :] = jnp.zeros((rows, buffer.shape[1]), BF16)

    def exchange_wait(buffer, phase):
        @pl.when(has_left)
        def _():
            halo(buffer, phase, 0).wait_send()
            halo(buffer, phase, 1).wait_recv()

        @pl.when(has_right)
        def _():
            halo(buffer, phase, 1).wait_send()
            halo(buffer, phase, 0).wait_recv()

    def convolve(buffer, weights, which):
        total[...] = jnp.zeros_like(total)

        def step(g, carry):
            weight_copy(which, g).wait()
            width = buffer.shape[1]
            for j in range(group):
                picked[:, j * width : (j + 1) * width] = jnp.dot(
                    select[g * group + j], buffer[...], preferred_element_type=F32
                ).astype(BF16)
            total[...] += jnp.dot(
                picked[...], weights[pl.ds(g * span, span), :], preferred_element_type=F32
            )
            return carry

        lax.fori_loop(0, steps, step, 0)
        return total[...]

    exchange_start(window, 0)

    @pl.when(has_right)
    def _():
        tally_copy().start()

    @pl.when(jnp.logical_not(has_left))
    def _():
        tally_in[...] = jnp.zeros_like(tally_in)
        sums_in[...] = jnp.zeros_like(sums_in)

    window[rows : 2 * rows] = features[...]
    exchange_wait(window, 0)
    middle[rows : 2 * rows] = settle(convolve(window, first, 0), gain_first[...]).astype(BF16)
    exchange_start(middle, 1)
    exchange_wait(middle, 1)
    fine = (features[...].astype(F32) + settle(convolve(middle, second, 1), gain_second[...])).astype(BF16)
    fine_out[...] = fine

    partial = jnp.dot(member, fine, preferred_element_type=F32)
    sums_out[...] = partial[par:]

    @pl.when(has_right)
    def _():
        sums_copy().start()

    for copy in small:
        copy.wait()

    @pl.when(has_right)
    def _():
        tally_copy().wait_send()
        sums_copy().wait_send()

    @pl.when(has_left)
    def _():
        tally_copy().wait_recv()
        sums_copy().wait_recv()

    counts = tallies[:par] + tally_in[:, :1]
    pooled = ((partial[:par] + sums_in[...]) / jnp.maximum(counts, 1.0)).astype(BF16)
    local = lax.dot_general(
        pooled, cot[...], (((0,), (0,)), ((), ())), preferred_element_type=F32
    )
    for k in range(chunks):
        r, c = (k // across) * chunk_rows, (k % across) * chunk_cols
        parts[k] = local[r : r + chunk_rows, c : c + chunk_cols].astype(BF16)

    mine = flat // stride
    owns = flat % stride == 0

    def part_copy(i):
        k = (mine + i) % chunks
        owner = k * stride
        return owner, pltpu.make_async_remote_copy(
            src_ref=parts.at[k],
            dst_ref=landed.at[(flat - owner - 1 + n) % n],
            send_sem=part_send,
            recv_sem=part_recv,
            device_id=place(owner),
            device_id_type=MESH,
        )

    def send_part(i, carry):
        part_copy(i)[1].start()
        return carry

    lax.fori_loop(1, chunks, send_part, 0)
    if stride > 1:

        @pl.when(jnp.logical_not(owns))
        def _():
            send_part(0, 0)

    coarse[...] = jnp.dot(pooled, down[...], preferred_element_type=F32).astype(BF16)

    def bulk(ref, count, send, recv):
        cut = ref.at[pl.ds(0, count)]
        return pltpu.make_async_remote_copy(
            src_ref=cut,
            dst_ref=cut,
            send_sem=send,
            recv_sem=recv,
            device_id=place((flat + 1) % n),
            device_id_type=MESH,
        )

    def share(i, carry):
        pltpu.make_async_remote_copy(
            src_ref=gathered.at[mine],
            dst_ref=gathered.at[mine],
            send_sem=all_send,
            recv_sem=all_recv,
            device_id=place((flat + i) % n),
            device_id_type=MESH,
        ).start()
        return carry

    def own():
        bulk(landed, n - 1, part_send, part_recv).wait_recv()
        mean = parts[mine].astype(F32)

        def add(i, running):
            return running + landed[i].astype(F32)

        mean = lax.fori_loop(0, n - 1, add, mean, unroll=True)
        gathered[mine] = (mean * scale).astype(BF16)
        lax.fori_loop(1, n, share, 0)
        bulk(parts, chunks - 1, part_send, part_recv).wait_send()
        bulk(gathered, chunks - 1, all_send, all_recv).wait_recv()
        bulk(landed, n - 1, all_send, all_recv).wait_send()

    def follow():
        bulk(parts, chunks, part_send, part_recv).wait_send()
        bulk(gathered, chunks, all_send, all_recv).wait_recv()

    if stride == 1:
        own()
    else:
        pl.when(owns)(own)
        pl.when(jnp.logical_not(owns))(follow)

    for k in range(chunks):
        r, c = (k // across) * chunk_rows, (k % across) * chunk_cols
        grad[r : r + chunk_rows, c : c + chunk_cols] = gathered[k]


def body(
    n_dp,
    n_space,
    features,
    neighbours,
    parents,
    conv_first,
    conv_second,
    gain_first,
    gain_second,
    down_weight,
    cotangent,
):
    worlds, rows, width = features.shape
    taps = neighbours.shape[1]
    par, out_width = cotangent.shape[1:]
    n = n_dp * n_space
    group = 9 if taps % 9 == 0 else 1
    chunks = min(n, (width // 16) * (out_width // 128))
    stride = n // chunks
    tall = min(chunks, width // 16)
    chunk_rows, chunk_cols = width // tall, out_width // (chunks // tall)
    scale = 1.0 / math.sqrt(worlds * n_dp * par * n_space)
    vmem = pl.BlockSpec(memory_space=pltpu.VMEM)
    hbm = pl.BlockSpec(memory_space=pl.ANY)
    dma = pltpu.SemaphoreType.DMA
    fine_out, coarse, grad = pl.pallas_call(
        functools.partial(kernel, (n_dp, n_space, taps, group, chunks, stride, scale)),
        out_shape=(
            jax.ShapeDtypeStruct((rows, width), BF16),
            jax.ShapeDtypeStruct((par, out_width), BF16),
            jax.ShapeDtypeStruct((width, out_width), BF16),
        ),
        in_specs=[vmem] * 5 + [hbm] * 4,
        out_specs=(vmem,) * 3,
        scratch_shapes=[
            pltpu.VMEM((3 * rows, width), BF16),
            pltpu.VMEM((3 * rows, width), BF16),
            pltpu.VMEM((taps, rows, 3 * rows), BF16),
            pltpu.VMEM((rows, group * width), BF16),
            pltpu.VMEM((taps * width, width), BF16),
            pltpu.VMEM((taps * width, width), BF16),
            pltpu.VMEM((width, out_width), BF16),
            pltpu.VMEM((par, out_width), BF16),
            pltpu.VMEM((rows, width), F32),
            pltpu.VMEM((par, width), F32),
            pltpu.VMEM((par, width), F32),
            pltpu.VMEM((par, 128), F32),
            pltpu.VMEM((par, 128), F32),
            pltpu.VMEM((chunks, chunk_rows, chunk_cols), BF16),
            pltpu.VMEM((n - 1, chunk_rows, chunk_cols), BF16),
            pltpu.VMEM((chunks, chunk_rows, chunk_cols), BF16),
            dma((2, taps // group)),
            dma((2,)),
            dma((2, 2)),
            dma((2, 2)),
            dma((2,)),
            dma((2,)),
            dma,
            dma,
            dma,
            dma,
        ],
        compiler_params=pltpu.CompilerParams(
            collective_id=0, has_side_effects=True, vmem_limit_bytes=60 * 2**20
        ),
    )(
        features[0],
        neighbours[0],
        parents,
        gain_first[None],
        gain_second[None],
        conv_first.reshape(taps * width, width),
        conv_second.reshape(taps * width, width),
        down_weight,
        cotangent[0],
    )
    return fine_out[None], coarse[None], grad.astype(F32)


def solution(mesh):
    return jax.shard_map(
        functools.partial(body, mesh.shape["dp"], mesh.shape["space"]),
        mesh=mesh,
        in_specs=(
            P("dp", "space", None),
            P("dp", None, "space"),
            P("dp", "space"),
            P(),
            P(),
            P(),
            P(),
            P(),
            P("dp", "space", None),
        ),
        out_specs=(P("dp", "space", None), P("dp", "space", None), P()),
        check_vma=False,
    )
```

```python
import functools
import math

import jax
import jax.numpy as jnp
from jax import lax
from jax.experimental import pallas as pl
from jax.experimental.pallas import tpu as pltpu
from jax.sharding import PartitionSpec as P

F32 = jnp.float32
BF16 = jnp.bfloat16
MESH = pl.DeviceIdType.MESH


def settle(total, gain):
    inverse = lax.rsqrt(jnp.mean(total * total, axis=-1, keepdims=True) + 1e-05)
    u = total * inverse * gain
    return u / (1.0 + jnp.exp(-u))


def kernel(
    shape,
    features,
    neighbours,
    parents,
    gain_first,
    gain_second,
    first_hbm,
    second_hbm,
    down_hbm,
    cot_hbm,
    fine_hbm,
    coarse_hbm,
    grad_hbm,
    window,
    middle,
    select,
    picked,
    first,
    second,
    down,
    cot,
    total,
    fine_out,
    coarse,
    sums_out,
    sums_in,
    tally_out,
    tally_in,
    parts,
    landed,
    gathered,
    weight_sem,
    small_sem,
    halo_send,
    halo_recv,
    sum_send,
    sum_recv,
    part_send,
    part_recv,
    all_send,
    all_recv,
    out_sem,
):
    n_dp, n_space, taps, group, chunks, stride, scale = shape
    n = n_dp * n_space
    rows = features.shape[0]
    par = cot.shape[0] // 2
    chunk_rows, chunk_cols = parts.shape[1:]
    across = cot.shape[1] // chunk_cols
    width = features.shape[1]
    me_dp, me = lax.axis_index("dp"), lax.axis_index("space")
    flat = me_dp * n_space + me

    def place(device):
        return (device // n_space, device % n_space)

    barrier = pltpu.get_barrier_semaphore()

    def greet(i, carry):
        pl.semaphore_signal(barrier, inc=1, device_id=place((flat + i) % n), device_id_type=MESH)
        return carry

    lax.fori_loop(1, n, greet, 0)

    span = group * first.shape[1]
    steps = taps // group

    def weight_copy(which, g):
        source, target = ((first_hbm, first), (second_hbm, second))[which]
        cut = pl.ds(g * span, span)
        return pltpu.make_async_copy(source.at[cut], target.at[cut], weight_sem.at[which, g])

    small = [
        pltpu.make_async_copy(down_hbm, down, small_sem.at[0]),
        pltpu.make_async_copy(cot_hbm, cot.at[pl.ds(0, par)], small_sem.at[1]),
    ]
    for copy in small:
        copy.start()
    for which in range(2):
        for g in range(steps):
            weight_copy(which, g).start()

    ids = neighbours[:, 0, :]
    lookup = jnp.where(ids < 0, -1, ids - (me - 1) * rows).astype(F32)
    columns = jnp.transpose(lookup)
    places = lax.broadcasted_iota(jnp.int32, (rows, 3 * rows), 1).astype(F32)
    for t in range(taps):
        hit = columns[:, t : t + 1] == places
        select[t] = jnp.where(hit, 1.0, 0.0).astype(BF16)

    parent_ids = me * par + lax.broadcasted_iota(jnp.int32, (2 * par, rows), 0)
    member = jnp.where(parents[...] == parent_ids, 1.0, 0.0)
    tallies = jnp.sum(member, axis=1, keepdims=True)
    tally_out[...] = jnp.broadcast_to(tallies, tally_out.shape)
    member = member.astype(BF16)

    pl.semaphore_wait(barrier, n - 1)

    has_left, has_right = me > 0, me < n_space - 1

    def halo(buffer, phase, side):
        source = features if buffer is window else buffer.at[pl.ds(rows, rows)]
        return pltpu.make_async_remote_copy(
            src_ref=source,
            dst_ref=buffer.at[pl.ds(2 * rows * (1 - side), rows)],
            send_sem=halo_send.at[phase, side],
            recv_sem=halo_recv.at[phase, side],
            device_id=(me_dp, me + (2 * side - 1)),
            device_id_type=MESH,
        )

    def to_side(source, target, slot, side):
        return pltpu.make_async_remote_copy(
            src_ref=source,
            dst_ref=target,
            send_sem=sum_send.at[slot],
            recv_sem=sum_recv.at[slot],
            device_id=(me_dp, me + (2 * side - 1)),
            device_id_type=MESH,
        )

    low, high = pl.ds(0, par), pl.ds(par, par)

    def sums_copy():
        return to_side(sums_out, sums_in, 0, 1)

    def count_right():
        return to_side(tally_out.at[high], tally_in.at[low], 1, 1)

    def count_left():
        return to_side(tally_out.at[low], tally_in.at[high], 2, 0)

    def cot_left():
        return to_side(cot.at[low], cot.at[high], 3, 0)

    def exchange_start(buffer, phase):
        @pl.when(has_left)
        def _():
            halo(buffer, phase, 0).start()

        @pl.when(has_right)
        def _():
            halo(buffer, phase, 1).start()

        @pl.when(jnp.logical_not(has_left))
        def _():
            buffer[:rows] = jnp.zeros((rows, buffer.shape[1]), BF16)

        @pl.when(jnp.logical_not(has_right))
        def _():
            buffer[2 * rows :] = jnp.zeros((rows, buffer.shape[1]), BF16)

    def arrive(phase, buffer, side):
        @pl.when((has_right, has_left)[side])
        def _():
            halo(buffer, phase, side).wait_recv()

    def sent(phase, buffer):
        for side, there in enumerate((has_left, has_right)):

            @pl.when(there)
            def _():
                halo(buffer, phase, side).wait_send()

    odd = me % 2

    def convolve(buffer, weights, which):
        def pick(stage, g):
            for j in range(group):
                spot = (rows, 2 * rows * (1 - odd), 2 * rows * odd)[stage]
                if stage:
                    spot = pl.multiple_of(spot, rows)
                t = g * group + j
                found = jnp.dot(
                    select[t, :, pl.ds(spot, rows)],
                    buffer[pl.ds(spot, rows), :],
                    preferred_element_type=F32,
                ).astype(BF16)
                cut = (g, slice(None), slice(j * width, (j + 1) * width))
                picked[cut] = picked[cut] + found if stage else found

        def early(stage):
            def step(g, carry):
                pick(stage, g)
                return carry

            lax.fori_loop(0, steps, step, 0)

        early(0)

        @pl.when(odd == 0)
        def _():
            arrive(which, buffer, 0)

        @pl.when(odd == 1)
        def _():
            arrive(which, buffer, 1)

        early(1)

        @pl.when(odd == 0)
        def _():
            arrive(which, buffer, 1)

        @pl.when(odd == 1)
        def _():
            arrive(which, buffer, 0)

        total[...] = jnp.zeros_like(total)

        def step(g, carry):
            pick(2, g)
            weight_copy(which, g).wait()
            total[...] += jnp.dot(
                picked[g], weights[pl.ds(g * span, span), :], preferred_element_type=F32
            )
            return carry

        lax.fori_loop(0, steps, step, 0)
        sent(which, buffer)
        return total[...]

    window[rows : 2 * rows] = features[...]
    exchange_start(window, 0)
    for copy in small:
        copy.wait()

    @pl.when(has_left)
    def _():
        count_left().start()
        cot_left().start()

    @pl.when(has_right)
    def _():
        count_right().start()

    @pl.when(jnp.logical_not(has_left))
    def _():
        tally_in[:par] = jnp.zeros((par, tally_in.shape[1]), F32)
        sums_in[...] = jnp.zeros_like(sums_in)

    @pl.when(jnp.logical_not(has_right))
    def _():
        tally_in[par:] = jnp.zeros((par, tally_in.shape[1]), F32)
        cot[par:] = jnp.zeros((par, cot.shape[1]), BF16)

    middle[rows : 2 * rows] = settle(convolve(window, first, 0), gain_first[...]).astype(BF16)
    exchange_start(middle, 1)

    @pl.when(has_left)
    def _():
        count_left().wait_send()
        cot_left().wait_send()
        count_right().wait_recv()

    @pl.when(has_right)
    def _():
        count_right().wait_send()
        count_left().wait_recv()
        cot_left().wait_recv()

    share_of = 1.0 / jnp.maximum(tallies + tally_in[:, :1], 1.0)
    fine = (features[...].astype(F32) + settle(convolve(middle, second, 1), gain_second[...])).astype(BF16)
    fine_out[...] = fine
    partial = jnp.dot(member, fine, preferred_element_type=F32)
    local = lax.dot_general(
        (partial * share_of).astype(BF16),
        cot[...],
        (((0,), (0,)), ((), ())),
        preferred_element_type=F32,
    )
    for k in range(chunks):
        r, c = (k // across) * chunk_rows, (k % across) * chunk_cols
        parts[k] = local[r : r + chunk_rows, c : c + chunk_cols].astype(BF16)

    mine = flat // stride
    owns = flat % stride == 0

    def part_copy(i):
        k = (mine + i) % chunks
        owner = k * stride
        return owner, pltpu.make_async_remote_copy(
            src_ref=parts.at[k],
            dst_ref=landed.at[(flat - owner - 1 + n) % n],
            send_sem=part_send,
            recv_sem=part_recv,
            device_id=place(owner),
            device_id_type=MESH,
        )

    def send_part(i, carry):
        part_copy(i)[1].start()
        return carry

    lax.fori_loop(1, chunks, send_part, 0)
    if stride > 1:

        @pl.when(jnp.logical_not(owns))
        def _():
            send_part(0, 0)

    outs = [
        pltpu.make_async_copy(fine_out, fine_hbm, out_sem.at[0]),
        pltpu.make_async_copy(coarse, coarse_hbm, out_sem.at[1]),
    ]
    outs[0].start()
    sums_out[...] = partial[par:]

    @pl.when(has_right)
    def _():
        sums_copy().start()
        sums_copy().wait_send()

    @pl.when(has_left)
    def _():
        sums_copy().wait_recv()

    pooled = ((partial[:par] + sums_in[...]) * share_of[:par]).astype(BF16)
    coarse[...] = jnp.dot(pooled, down[...], preferred_element_type=F32).astype(BF16)
    outs[1].start()

    def bulk(ref, count, send, recv):
        cut = ref.at[pl.ds(0, count)]
        return pltpu.make_async_remote_copy(
            src_ref=cut,
            dst_ref=cut,
            send_sem=send,
            recv_sem=recv,
            device_id=place((flat + 1) % n),
            device_id_type=MESH,
        )

    def share(i, carry):
        pltpu.make_async_remote_copy(
            src_ref=gathered.at[mine],
            dst_ref=gathered.at[mine],
            send_sem=all_send,
            recv_sem=all_recv,
            device_id=place((flat + i) % n),
            device_id_type=MESH,
        ).start()
        return carry

    def own():
        bulk(landed, n - 1, part_send, part_recv).wait_recv()
        mean = parts[mine].astype(F32)

        def add(i, running):
            return running + landed[i].astype(F32)

        mean = lax.fori_loop(0, n - 1, add, mean, unroll=True)
        gathered[mine] = (mean * scale).astype(BF16)
        lax.fori_loop(1, n, share, 0)
        bulk(parts, chunks - 1, part_send, part_recv).wait_send()
        bulk(gathered, chunks - 1, all_send, all_recv).wait_recv()
        bulk(landed, n - 1, all_send, all_recv).wait_send()

    def follow():
        bulk(parts, chunks, part_send, part_recv).wait_send()
        bulk(gathered, chunks, all_send, all_recv).wait_recv()

    if stride == 1:
        own()
    else:
        pl.when(owns)(own)
        pl.when(jnp.logical_not(owns))(follow)

    last = pltpu.make_async_copy(gathered, grad_hbm, out_sem.at[2])
    last.start()
    for copy in outs:
        copy.wait()
    last.wait()


def finish(fine, coarse, gathered, fine_out, coarse_out, grad):
    chunks, chunk_rows, chunk_cols = gathered.shape
    across = grad.shape[1] // chunk_cols
    fine_out[...] = fine[...]
    coarse_out[...] = coarse[...]
    for k in range(chunks):
        r, c = (k // across) * chunk_rows, (k % across) * chunk_cols
        grad[r : r + chunk_rows, c : c + chunk_cols] = gathered[k].astype(F32)


def body(
    n_dp,
    n_space,
    features,
    neighbours,
    parents,
    conv_first,
    conv_second,
    gain_first,
    gain_second,
    down_weight,
    cotangent,
):
    worlds, rows, width = features.shape
    taps = neighbours.shape[1]
    par, out_width = cotangent.shape[1:]
    n = n_dp * n_space
    group = 9 if taps % 9 == 0 else 1
    chunks = min(n, (width // 16) * (out_width // 128))
    stride = n // chunks
    tall = min(chunks, width // 16)
    chunk_rows, chunk_cols = width // tall, out_width // (chunks // tall)
    scale = 1.0 / math.sqrt(worlds * n_dp * par * n_space)
    vmem = pl.BlockSpec(memory_space=pltpu.VMEM)
    hbm = pl.BlockSpec(memory_space=pl.ANY)
    dma = pltpu.SemaphoreType.DMA
    fine_out, coarse, grad = pl.pallas_call(
        functools.partial(kernel, (n_dp, n_space, taps, group, chunks, stride, scale)),
        out_shape=(
            jax.ShapeDtypeStruct((rows, width), BF16),
            jax.ShapeDtypeStruct((par, out_width), BF16),
            jax.ShapeDtypeStruct((chunks, chunk_rows, chunk_cols), BF16),
        ),
        in_specs=[vmem] * 5 + [hbm] * 4,
        out_specs=(hbm,) * 3,
        scratch_shapes=[
            pltpu.VMEM((3 * rows, width), BF16),
            pltpu.VMEM((3 * rows, width), BF16),
            pltpu.VMEM((taps, rows, 3 * rows), BF16),
            pltpu.VMEM((taps // group, rows, group * width), BF16),
            pltpu.VMEM((taps * width, width), BF16),
            pltpu.VMEM((taps * width, width), BF16),
            pltpu.VMEM((width, out_width), BF16),
            pltpu.VMEM((2 * par, out_width), BF16),
            pltpu.VMEM((rows, width), F32),
            pltpu.VMEM((rows, width), BF16),
            pltpu.VMEM((par, out_width), BF16),
            pltpu.VMEM((par, width), F32),
            pltpu.VMEM((par, width), F32),
            pltpu.VMEM((2 * par, 128), F32),
            pltpu.VMEM((2 * par, 128), F32),
            pltpu.VMEM((chunks, chunk_rows, chunk_cols), BF16),
            pltpu.VMEM((n - 1, chunk_rows, chunk_cols), BF16),
            pltpu.VMEM((chunks, chunk_rows, chunk_cols), BF16),
            dma((2, taps // group)),
            dma((2,)),
            dma((2, 2)),
            dma((2, 2)),
            dma((4,)),
            dma((4,)),
            dma,
            dma,
            dma,
            dma,
            dma((3,)),
        ],
        compiler_params=pltpu.CompilerParams(
            collective_id=0, has_side_effects=True, vmem_limit_bytes=60 * 2**20
        ),
    )(
        features[0],
        jnp.transpose(neighbours, (1, 0, 2)),
        parents,
        gain_first[None],
        gain_second[None],
        conv_first.reshape(taps * width, width),
        conv_second.reshape(taps * width, width),
        down_weight,
        cotangent[0],
    )
    fine_out, coarse, grad = pl.pallas_call(
        finish,
        out_shape=(
            jax.ShapeDtypeStruct((rows, width), BF16),
            jax.ShapeDtypeStruct((par, out_width), BF16),
            jax.ShapeDtypeStruct((width, out_width), F32),
        ),
        in_specs=[vmem] * 3,
        out_specs=(vmem,) * 3,
    )(fine_out, coarse, grad)
    return fine_out[None], coarse[None], grad


def solution(mesh):
    return jax.shard_map(
        functools.partial(body, mesh.shape["dp"], mesh.shape["space"]),
        mesh=mesh,
        in_specs=(
            P("dp", "space", None),
            P("dp", None, "space"),
            P("dp", "space"),
            P(),
            P(),
            P(),
            P(),
            P(),
            P("dp", "space", None),
        ),
        out_specs=(P("dp", "space", None), P("dp", "space", None), P()),
        check_vma=False,
    )
```

```python
import functools
import math

import jax
import jax.numpy as jnp
from jax import lax
from jax.experimental import pallas as pl
from jax.experimental.pallas import tpu as pltpu
from jax.sharding import PartitionSpec as P

F32 = jnp.float32
BF16 = jnp.bfloat16
MESH = pl.DeviceIdType.MESH


def settle(total, gain):
    inverse = lax.rsqrt(jnp.mean(total * total, axis=-1, keepdims=True) + 1e-05)
    u = total * inverse * gain
    return u / (1.0 + jnp.exp(-u))


def kernel(
    shape,
    features_hbm,
    neighbours_hbm,
    parents_hbm,
    gain_first_hbm,
    gain_second_hbm,
    first_hbm,
    second_hbm,
    down_hbm,
    cot_hbm,
    fine_hbm,
    coarse_hbm,
    grad_hbm,
    features,
    neighbours,
    parents,
    gain_first,
    gain_second,
    window,
    middle,
    select,
    picked,
    first,
    second,
    down,
    cot,
    total,
    fine_out,
    coarse,
    sums_out,
    sums_in,
    tally_out,
    tally_in,
    parts,
    swap,
    merged,
    landed,
    gathered,
    weight_sem,
    small_sem,
    halo_send,
    halo_recv,
    sum_send,
    sum_recv,
    part_send,
    part_recv,
    all_send,
    all_recv,
    out_sem,
    swap_send,
    swap_recv,
    input_sem,
):
    n_dp, n_space, taps, group, chunks, stride, scale = shape
    n = n_dp * n_space
    rows = features.shape[0]
    par = cot.shape[0] // 2
    chunk_rows, chunk_cols = parts.shape[2:]
    across = cot.shape[1] // chunk_cols
    width = features.shape[1]
    me_dp, me = lax.axis_index("dp"), lax.axis_index("space")
    flat = me_dp * n_space + me

    def place(device):
        return (device // n_space, device % n_space)

    barrier = pltpu.get_barrier_semaphore()

    def greet(i, carry):
        pl.semaphore_signal(barrier, inc=1, device_id=place((flat + i) % n), device_id_type=MESH)
        return carry

    lax.fori_loop(1, n, greet, 0)

    span = group * first.shape[1]
    steps = taps // group

    def weight_copy(which, g):
        source, target = ((first_hbm, first), (second_hbm, second))[which]
        cut = pl.ds(g * span, span)
        return pltpu.make_async_copy(source.at[cut], target.at[cut], weight_sem.at[which, g])

    inputs = [
        pltpu.make_async_copy(source, target, input_sem.at[i])
        for i, (source, target) in enumerate(
            (
                (neighbours_hbm, neighbours),
                (parents_hbm, parents),
                (features_hbm, features),
                (gain_first_hbm, gain_first),
                (gain_second_hbm, gain_second),
            )
        )
    ]
    small = [
        pltpu.make_async_copy(down_hbm, down, small_sem.at[0]),
        pltpu.make_async_copy(cot_hbm, cot.at[pl.ds(0, par)], small_sem.at[1]),
    ]
    for copy in inputs + small:
        copy.start()
    for which in range(2):
        for g in range(steps):
            weight_copy(which, g).start()

    for copy in inputs:
        copy.wait()
    ids = neighbours[:, 0, :]
    lookup = jnp.where(ids < 0, -1, ids - (me - 1) * rows).astype(F32)
    columns = jnp.transpose(lookup)
    places = lax.broadcasted_iota(jnp.int32, (rows, 3 * rows), 1).astype(F32)
    for t in range(taps):
        hit = columns[:, t : t + 1] == places
        select[t] = jnp.where(hit, 1.0, 0.0).astype(BF16)

    parent_ids = me * par + lax.broadcasted_iota(jnp.int32, (2 * par, rows), 0)
    member = jnp.where(parents[...] == parent_ids, 1.0, 0.0)
    tallies = jnp.sum(member, axis=1, keepdims=True)
    tally_out[...] = jnp.broadcast_to(tallies, tally_out.shape)
    member = member.astype(BF16)

    pl.semaphore_wait(barrier, n - 1)

    has_left, has_right = me > 0, me < n_space - 1

    def halo(buffer, phase, side):
        source = features if buffer is window else buffer.at[pl.ds(rows, rows)]
        return pltpu.make_async_remote_copy(
            src_ref=source,
            dst_ref=buffer.at[pl.ds(2 * rows * (1 - side), rows)],
            send_sem=halo_send.at[phase, side],
            recv_sem=halo_recv.at[phase, side],
            device_id=(me_dp, me + (2 * side - 1)),
            device_id_type=MESH,
        )

    def to_side(source, target, slot, side):
        return pltpu.make_async_remote_copy(
            src_ref=source,
            dst_ref=target,
            send_sem=sum_send.at[slot],
            recv_sem=sum_recv.at[slot],
            device_id=(me_dp, me + (2 * side - 1)),
            device_id_type=MESH,
        )

    low, high = pl.ds(0, par), pl.ds(par, par)

    def sums_copy():
        return to_side(sums_out, sums_in, 0, 1)

    def count_right():
        return to_side(tally_out.at[high], tally_in.at[low], 1, 1)

    def count_left():
        return to_side(tally_out.at[low], tally_in.at[high], 2, 0)

    def cot_left():
        return to_side(cot.at[low], cot.at[high], 3, 0)

    def exchange_start(buffer, phase):
        @pl.when(has_left)
        def _():
            halo(buffer, phase, 0).start()

        @pl.when(has_right)
        def _():
            halo(buffer, phase, 1).start()

        @pl.when(jnp.logical_not(has_left))
        def _():
            buffer[:rows] = jnp.zeros((rows, buffer.shape[1]), BF16)

        @pl.when(jnp.logical_not(has_right))
        def _():
            buffer[2 * rows :] = jnp.zeros((rows, buffer.shape[1]), BF16)

    def arrive(phase, buffer, side):
        @pl.when((has_right, has_left)[side])
        def _():
            halo(buffer, phase, side).wait_recv()

    def sent(phase, buffer):
        for side, there in enumerate((has_left, has_right)):

            @pl.when(there)
            def _():
                halo(buffer, phase, side).wait_send()

    odd = me % 2
    half = chunks // 2

    def convolve(buffer, weights, which):
        def pick(stage, g):
            for j in range(group):
                spot = (rows, 2 * rows * (1 - odd), 2 * rows * odd)[stage]
                if stage:
                    spot = pl.multiple_of(spot, rows)
                t = g * group + j
                found = jnp.dot(
                    select[t, :, pl.ds(spot, rows)],
                    buffer[pl.ds(spot, rows), :],
                    preferred_element_type=F32,
                ).astype(BF16)
                cut = (g, slice(None), slice(j * width, (j + 1) * width))
                picked[cut] = picked[cut] + found if stage else found

        def early(stage):
            def step(g, carry):
                pick(stage, g)
                return carry

            lax.fori_loop(0, steps, step, 0)

        early(0)

        @pl.when(odd == 0)
        def _():
            arrive(which, buffer, 0)

        @pl.when(odd == 1)
        def _():
            arrive(which, buffer, 1)

        early(1)

        @pl.when(odd == 0)
        def _():
            arrive(which, buffer, 1)

        @pl.when(odd == 1)
        def _():
            arrive(which, buffer, 0)

        total[...] = jnp.zeros_like(total)

        def step(g, carry):
            pick(2, g)
            weight_copy(which, g).wait()
            total[...] += jnp.dot(
                picked[g], weights[pl.ds(g * span, span), :], preferred_element_type=F32
            )
            return carry

        lax.fori_loop(0, steps, step, 0)
        sent(which, buffer)
        return total[...]

    window[rows : 2 * rows] = features[...]
    exchange_start(window, 0)
    for copy in small:
        copy.wait()

    @pl.when(has_left)
    def _():
        count_left().start()
        cot_left().start()

    @pl.when(has_right)
    def _():
        count_right().start()

    @pl.when(jnp.logical_not(has_left))
    def _():
        tally_in[:par] = jnp.zeros((par, tally_in.shape[1]), F32)
        sums_in[...] = jnp.zeros_like(sums_in)

    @pl.when(jnp.logical_not(has_right))
    def _():
        tally_in[par:] = jnp.zeros((par, tally_in.shape[1]), F32)
        cot[par:] = jnp.zeros((par, cot.shape[1]), BF16)

    middle[rows : 2 * rows] = settle(convolve(window, first, 0), gain_first[...]).astype(BF16)
    exchange_start(middle, 1)

    @pl.when(has_left)
    def _():
        count_left().wait_send()
        cot_left().wait_send()
        count_right().wait_recv()

    @pl.when(has_right)
    def _():
        count_right().wait_send()
        count_left().wait_recv()
        cot_left().wait_recv()

    share_of = 1.0 / jnp.maximum(tallies + tally_in[:, :1], 1.0)
    fine = (features[...].astype(F32) + settle(convolve(middle, second, 1), gain_second[...])).astype(BF16)
    fine_out[...] = fine
    partial = jnp.dot(member, fine, preferred_element_type=F32)
    local = lax.dot_general(
        (partial * share_of).astype(BF16),
        cot[...],
        (((0,), (0,)), ((), ())),
        preferred_element_type=F32,
    )
    for k in range(chunks):
        r, c = (k // across) * chunk_rows, (k % across) * chunk_cols
        parts[k // half, k % half] = local[r : r + chunk_rows, c : c + chunk_cols].astype(BF16)

    team = n // 2
    spot = flat // 2
    mine = spot // stride
    owns = spot % stride == 0

    def mate(i):
        return place(((spot + i) % team) * 2 + odd)

    def trade(source, target, slot):
        return pltpu.make_async_remote_copy(
            src_ref=source,
            dst_ref=target,
            send_sem=swap_send.at[slot],
            recv_sem=swap_recv.at[slot],
            device_id=place(flat + 1 - 2 * odd),
            device_id_type=MESH,
        )

    halves = trade(parts.at[1 - odd], swap, 0)
    halves.start()
    sums_out[...] = partial[par:]

    @pl.when(has_right)
    def _():
        sums_copy().start()

    halves.wait()
    merged[...] = (parts[odd].astype(F32) + swap[...].astype(F32)).astype(BF16)

    def send_part(i, carry):
        k = (mine + i) % half
        owner = k * stride
        pltpu.make_async_remote_copy(
            src_ref=merged.at[k],
            dst_ref=landed.at[(spot - owner - 1 + team) % team],
            send_sem=part_send,
            recv_sem=part_recv,
            device_id=place(owner * 2 + odd),
            device_id_type=MESH,
        ).start()
        return carry

    lax.fori_loop(1, half, send_part, 0)
    if stride > 1:

        @pl.when(jnp.logical_not(owns))
        def _():
            send_part(0, 0)

    outs = [
        pltpu.make_async_copy(fine_out, fine_hbm, out_sem.at[0]),
        pltpu.make_async_copy(coarse, coarse_hbm, out_sem.at[1]),
    ]
    outs[0].start()
    @pl.when(has_right)
    def _():
        sums_copy().wait_send()

    @pl.when(has_left)
    def _():
        sums_copy().wait_recv()

    pooled = ((partial[:par] + sums_in[...]) * share_of[:par]).astype(BF16)
    coarse[...] = jnp.dot(pooled, down[...], preferred_element_type=F32).astype(BF16)
    outs[1].start()

    def bulk(ref, count, send, recv):
        cut = ref.at[pl.ds(0, count)]
        return pltpu.make_async_remote_copy(
            src_ref=cut,
            dst_ref=cut,
            send_sem=send,
            recv_sem=recv,
            device_id=mate(1),
            device_id_type=MESH,
        )

    def share(i, carry):
        pltpu.make_async_remote_copy(
            src_ref=gathered.at[odd, mine],
            dst_ref=gathered.at[odd, mine],
            send_sem=all_send,
            recv_sem=all_recv,
            device_id=mate(i),
            device_id_type=MESH,
        ).start()
        return carry

    def own():
        bulk(landed, team - 1, part_send, part_recv).wait_recv()
        mean = merged[mine].astype(F32)

        def add(i, running):
            return running + landed[i].astype(F32)

        mean = lax.fori_loop(0, team - 1, add, mean, unroll=True)
        gathered[odd, mine] = (mean * scale).astype(BF16)
        lax.fori_loop(1, team, share, 0)
        bulk(merged, half - 1, part_send, part_recv).wait_send()
        bulk(gathered.at[odd], half - 1, all_send, all_recv).wait_recv()
        bulk(landed, team - 1, all_send, all_recv).wait_send()

    def follow():
        bulk(merged, half, part_send, part_recv).wait_send()
        bulk(gathered.at[odd], half, all_send, all_recv).wait_recv()

    if stride == 1:
        own()
    else:
        pl.when(owns)(own)
        pl.when(jnp.logical_not(owns))(follow)

    whole = trade(gathered.at[odd], gathered.at[odd], 1)
    whole.start()
    whole.wait()
    last = pltpu.make_async_copy(gathered, grad_hbm, out_sem.at[2])
    last.start()
    for copy in outs:
        copy.wait()
    last.wait()


def finish(fine, coarse, gathered, fine_out, coarse_out, grad):
    _, half, chunk_rows, chunk_cols = gathered.shape
    across = grad.shape[1] // chunk_cols
    fine_out[...] = fine[...]
    coarse_out[...] = coarse[...]
    for k in range(2 * half):
        r, c = (k // across) * chunk_rows, (k % across) * chunk_cols
        grad[r : r + chunk_rows, c : c + chunk_cols] = gathered[k // half, k % half].astype(F32)


def body(
    n_dp,
    n_space,
    features,
    neighbours,
    parents,
    conv_first,
    conv_second,
    gain_first,
    gain_second,
    down_weight,
    cotangent,
):
    worlds, rows, width = features.shape
    taps = neighbours.shape[1]
    par, out_width = cotangent.shape[1:]
    n = n_dp * n_space
    group = 9 if taps % 9 == 0 else 1
    chunks = min(n, (width // 16) * (out_width // 128))
    stride = n // chunks
    tall = min(chunks, width // 16)
    chunk_rows, chunk_cols = width // tall, out_width // (chunks // tall)
    scale = 1.0 / math.sqrt(worlds * n_dp * par * n_space)
    vmem = pl.BlockSpec(memory_space=pltpu.VMEM)
    hbm = pl.BlockSpec(memory_space=pl.ANY)
    dma = pltpu.SemaphoreType.DMA
    fine_out, coarse, grad = pl.pallas_call(
        functools.partial(kernel, (n_dp, n_space, taps, group, chunks, stride, scale)),
        out_shape=(
            jax.ShapeDtypeStruct((rows, width), BF16),
            jax.ShapeDtypeStruct((par, out_width), BF16),
            jax.ShapeDtypeStruct((2, chunks // 2, chunk_rows, chunk_cols), BF16),
        ),
        in_specs=[hbm] * 9,
        out_specs=(hbm,) * 3,
        scratch_shapes=[
            pltpu.VMEM((rows, width), BF16),
            pltpu.VMEM((taps, 1, rows), jnp.int32),
            pltpu.VMEM((1, rows), jnp.int32),
            pltpu.VMEM((1, width), F32),
            pltpu.VMEM((1, width), F32),
            pltpu.VMEM((3 * rows, width), BF16),
            pltpu.VMEM((3 * rows, width), BF16),
            pltpu.VMEM((taps, rows, 3 * rows), BF16),
            pltpu.VMEM((taps // group, rows, group * width), BF16),
            pltpu.VMEM((taps * width, width), BF16),
            pltpu.VMEM((taps * width, width), BF16),
            pltpu.VMEM((width, out_width), BF16),
            pltpu.VMEM((2 * par, out_width), BF16),
            pltpu.VMEM((rows, width), F32),
            pltpu.VMEM((rows, width), BF16),
            pltpu.VMEM((par, out_width), BF16),
            pltpu.VMEM((par, width), F32),
            pltpu.VMEM((par, width), F32),
            pltpu.VMEM((2 * par, 128), F32),
            pltpu.VMEM((2 * par, 128), F32),
            pltpu.VMEM((2, chunks // 2, chunk_rows, chunk_cols), BF16),
            pltpu.VMEM((chunks // 2, chunk_rows, chunk_cols), BF16),
            pltpu.VMEM((chunks // 2, chunk_rows, chunk_cols), BF16),
            pltpu.VMEM((n // 2 - 1, chunk_rows, chunk_cols), BF16),
            pltpu.VMEM((2, chunks // 2, chunk_rows, chunk_cols), BF16),
            dma((2, taps // group)),
            dma((2,)),
            dma((2, 2)),
            dma((2, 2)),
            dma((4,)),
            dma((4,)),
            dma,
            dma,
            dma,
            dma,
            dma((3,)),
            dma((2,)),
            dma((2,)),
            dma((5,)),
        ],
        compiler_params=pltpu.CompilerParams(
            collective_id=0, has_side_effects=True, vmem_limit_bytes=60 * 2**20
        ),
    )(
        features[0],
        jnp.transpose(neighbours, (1, 0, 2)),
        parents,
        gain_first[None],
        gain_second[None],
        conv_first.reshape(taps * width, width),
        conv_second.reshape(taps * width, width),
        down_weight,
        cotangent[0],
    )
    fine_out, coarse, grad = pl.pallas_call(
        finish,
        out_shape=(
            jax.ShapeDtypeStruct((rows, width), BF16),
            jax.ShapeDtypeStruct((par, out_width), BF16),
            jax.ShapeDtypeStruct((width, out_width), F32),
        ),
        in_specs=[vmem] * 3,
        out_specs=(vmem,) * 3,
    )(fine_out, coarse, grad)
    return fine_out[None], coarse[None], grad


def solution(mesh):
    return jax.shard_map(
        functools.partial(body, mesh.shape["dp"], mesh.shape["space"]),
        mesh=mesh,
        in_specs=(
            P("dp", "space", None),
            P("dp", None, "space"),
            P("dp", "space"),
            P(),
            P(),
            P(),
            P(),
            P(),
            P("dp", "space", None),
        ),
        out_specs=(P("dp", "space", None), P("dp", "space", None), P()),
        check_vma=False,
    )
```
